32 devices in a mesh: prow: 4 (over y, x), pcol: 8 (over z, core).
Axes of the slice: x: 2, y: 2, z: 4, core: 2. Of those that a mesh axis runs over, the one named last changes fastest.
Arguments:
- region_inverse: float32 [2, 12288, 12288], P(None, 'prow', 'pcol'), may hold values from -1.25 to 1.25
- panel_a: float32 [2, 12288, 256], P(None, ('prow', 'pcol')), may hold values from -0.109375 to 0.109375
- panel_b: float32 [2, 12288, 256], P(None, ('prow', 'pcol')), may hold values from -0.109375 to 0.109375
- top_block: float32 [2, 256, 256], P(None, 'pcol'), may hold values from -0.25 to 0.25
- diag_a: float32 [2, 256, 256], P(None, 'pcol'), may hold values from -6 to 6
- diag_b: float32 [2, 256, 256], P(None, 'pcol'), may hold values from -6 to 6
- block_rows: int32 [96], replicated, may hold values from 32 to 128, as said below
- struct_b: int32 [48], replicated, may hold values from 0 to 95, as said below
Outputs:
- column_a: float32 [2, 12288, 256], P(None, ('prow', 'pcol'))
- corner_a: float32 [2, 256, 256], replicated
- top_b: float32 [2, 256, 256], replicated
- column_b: float32 [2, 12288, 256], P(None, ('prow', 'pcol'))
- corner_b: float32 [2, 256, 256], replicated
The draws below stay inside these ranges and needn't reach their ends.
Inputs may be any that keep to these rules, and one draw needn't show every extreme that they name: `block_rows`: each block has 32 to 128 live rows; some block is full. `struct_b`: distinct and increasing; always holds block 0 and block 95.
All inputs are finite; a program needn't handle non-finite values.
Results may differ from the reference program's by a relative error of at most 0.0001.
Values sent between devices are 32-bit elements; how exact they have to be, the bound alone decides.
No kernel may reach another device: no remote copies, remote signals or barrier semaphores. Data moves between devices by JAX's collectives and lax.ppermute only.
A program may use at most 192 MiB of HBM per device.

```python
import jax
import jax.numpy as jnp
from jax import lax

NB = 96
BS = 128
W = 256
SB = 48


def draw_block_rows(key, part):
    heights = jax.random.randint(jax.random.fold_in(key, 11), (NB,), BS // 4, BS + 1)
    tallest = jax.random.randint(jax.random.fold_in(key, 12), (), 0, NB)
    return jnp.where(jnp.arange(NB) == tallest, BS, heights).astype(jnp.int32)


def draw_struct_b(key, part):
    shuffled = jax.random.permutation(jax.random.fold_in(key, 13), NB - 2).astype(jnp.int32) + 1
    chosen = shuffled[:SB - 2]
    members = jnp.concatenate([jnp.array([0, NB - 1], dtype=jnp.int32), chosen])
    return jnp.sort(members).astype(jnp.int32)


def level_of(own_key, extent, split, least, top_value):
    gain = 1.0
    for dim, shards_of in split:
        steps = jax.random.uniform(jax.random.fold_in(jax.random.fold_in(own_key, 6), dim), (shards_of,), jnp.float32, least / len(split), top_value / len(split))
        gain = gain * jnp.repeat(jnp.exp(steps), extent[dim] // shards_of).reshape((-1,) + (1,) * (len(extent) - 1 - dim))
    return gain


def gaussian(key, shape, scale, most, pieces=(), kind=jnp.bfloat16):
    level = level_of(key, shape, pieces, -0.22, 0.18) if pieces else 1.0
    values = jax.random.normal(key, shape, jnp.float32) * scale * level
    return jnp.minimum(jnp.maximum(values, -most), most).astype(kind)


def setup_inputs(seed: int = 0) -> dict:
    splits = jax.random.split(jax.random.key(seed), 9)
    return {
        "region_inverse": gaussian(splits[0], (2, NB * BS, NB * BS), 0.2, 1.25, ((1, 4), (2, 8)), jnp.float32),
        "panel_a": gaussian(splits[1], (2, NB * BS, W), (NB * BS // 4) ** -0.5, 0.109375, ((1, 32),), jnp.float32),
        "panel_b": gaussian(splits[2], (2, NB * BS, W), (NB * BS // 4) ** -0.5, 0.109375, ((1, 32),), jnp.float32),
        "top_block": gaussian(splits[3], (2, W, W), (2 * W) ** -0.5, 0.25, ((1, 8),), jnp.float32),
        "diag_a": gaussian(splits[4], (2, W, W), 1.0, 6.0, ((1, 8),), jnp.float32),
        "diag_b": gaussian(splits[5], (2, W, W), 1.0, 6.0, ((1, 8),), jnp.float32),
        "block_rows": draw_block_rows(jax.random.fold_in(splits[8], 71), 0),
        "struct_b": draw_struct_b(jax.random.fold_in(splits[8], 71), 0),
    }


def complex_product(left, right):
    highest = lax.Precision.HIGHEST
    real_part = jnp.dot(left[0], right[0], precision=highest, preferred_element_type=jnp.float32) - jnp.dot(left[1], right[1], precision=highest, preferred_element_type=jnp.float32)
    imag_part = jnp.dot(left[0], right[1], precision=highest, preferred_element_type=jnp.float32) + jnp.dot(left[1], right[0], precision=highest, preferred_element_type=jnp.float32)
    return jnp.stack([real_part, imag_part])


def flipped(matrix):
    return jnp.swapaxes(matrix, 1, 2)


def row_limits(block_rows, struct_b):
    positions = jnp.arange(NB * BS, dtype=jnp.int32)
    block_ids = positions // BS
    within = positions % BS
    live_rows = within < block_rows[block_ids]
    member = jnp.any(struct_b[:, None] == jnp.arange(NB, dtype=jnp.int32)[None, :], axis=0)
    return live_rows, live_rows & member[block_ids]


def reference(region_inverse, panel_a, panel_b, top_block, diag_a, diag_b, block_rows, struct_b):
    live_rows, kept_rows = row_limits(block_rows, struct_b)
    live_mask = live_rows[None, :, None]
    kept_mask = kept_rows[None, :, None]
    masked_a = jnp.where(live_mask, panel_a, 0.0)
    masked_b = jnp.where(kept_mask, panel_b, 0.0)
    column_a = -jnp.where(live_mask, complex_product(region_inverse, masked_a), 0.0)
    column_b = -jnp.where(kept_mask, complex_product(region_inverse, masked_b) + complex_product(column_a, top_block), 0.0)
    corner_a = diag_a - complex_product(flipped(masked_a), column_a)
    top_b = -(complex_product(corner_a, top_block) + complex_product(flipped(column_a), masked_b))
    corner_b = diag_b - complex_product(flipped(top_block), top_b) - complex_product(flipped(masked_b), column_b)
    return column_a, corner_a, top_b, column_b, corner_b
```

```python
import jax
import jax.numpy as jnp
from jax import lax
from jax.experimental import pallas as pl
from jax.experimental.pallas import tpu as pltpu
from jax.sharding import PartitionSpec as P

BS = 128
GROUP = 16
AXES = ("prow", "pcol")
HIGH = lax.Precision.HIGH


def spread(block, axis, owner):
    block = jnp.where(lax.axis_index(axis) == owner, block, jnp.zeros_like(block))
    return lax.psum(block, axis)


def complex_product(left, right):
    highest = lax.Precision.HIGHEST
    real_part = jnp.dot(
        left[0], right[0], precision=highest, preferred_element_type=jnp.float32
    ) - jnp.dot(left[1], right[1], precision=highest, preferred_element_type=jnp.float32)
    imag_part = jnp.dot(
        left[0], right[1], precision=highest, preferred_element_type=jnp.float32
    ) + jnp.dot(left[1], right[0], precision=highest, preferred_element_type=jnp.float32)
    return jnp.stack([real_part, imag_part])


def flipped(matrix):
    return jnp.swapaxes(matrix, 1, 2)


def limits_for(block_rows, struct_b, start, count):
    positions = start + jnp.arange(count, dtype=jnp.int32)
    block_ids = positions // BS
    within = positions % BS
    catalog = jnp.arange(block_rows.shape[0], dtype=jnp.int32)
    selector = block_ids[:, None] == catalog[None, :]
    heights = jnp.sum(jnp.where(selector, block_rows[None, :], 0), axis=1)
    member = jnp.any(struct_b[:, None] == catalog[None, :], axis=0)
    chosen = jnp.any(selector & member[None, :], axis=1)
    live_rows = within < heights
    return (live_rows, live_rows & chosen)


def region_terms(region_inverse, columns_real, columns_imag):
    highest = lax.Precision.HIGHEST
    block_real = region_inverse[0]
    block_imag = region_inverse[1]
    real_part = jnp.dot(
        block_real, columns_real, precision=highest, preferred_element_type=jnp.float32
    ) - jnp.dot(block_imag, columns_imag, precision=highest, preferred_element_type=jnp.float32)
    imag_part = jnp.dot(
        block_real, columns_imag, precision=highest, preferred_element_type=jnp.float32
    ) + jnp.dot(block_imag, columns_real, precision=highest, preferred_element_type=jnp.float32)
    return jnp.concatenate([real_part, imag_part], axis=1)


def on_device_generic(region_inverse, panel_a, panel_b, top_block, diag_a, diag_b, block_rows, struct_b):
    own_rows = panel_a.shape[1]
    width = panel_a.shape[2]
    col_count = region_inverse.shape[2]
    range_a, range_b, top_full, full_diag_a, full_diag_b = (
        lax.all_gather(panel_a, "pcol", axis=1, tiled=True),
        lax.all_gather(panel_b, "pcol", axis=1, tiled=True),
        lax.all_gather(top_block, "pcol", axis=1, tiled=True),
        lax.all_gather(diag_a, "pcol", axis=1, tiled=True),
        lax.all_gather(diag_b, "pcol", axis=1, tiled=True),
    )
    col_index = lax.axis_index("pcol")
    row_index = lax.axis_index("prow")
    ratio = lax.axis_size("pcol") // lax.axis_size("prow")
    section = col_index % ratio
    slice_a = lax.dynamic_slice_in_dim(range_a, section * col_count, col_count, 1)
    slice_b = lax.dynamic_slice_in_dim(range_b, section * col_count, col_count, 1)
    cols_a, cols_b = (
        spread(slice_a, "prow", col_index // ratio),
        spread(slice_b, "prow", col_index // ratio),
    )
    col_live, col_kept = limits_for(block_rows, struct_b, col_index * col_count, col_count)
    cols_a = jnp.where(col_live[None, :, None], cols_a, 0.0)
    cols_b = jnp.where(col_kept[None, :, None], cols_b, 0.0)
    own_start = (row_index * lax.axis_size("pcol") + col_index) * own_rows
    own_live, own_kept = limits_for(block_rows, struct_b, own_start, own_rows)
    live_mask = own_live[None, :, None]
    kept_mask = own_kept[None, :, None]
    masked_a = jnp.where(live_mask, panel_a, 0.0)
    masked_b = jnp.where(kept_mask, panel_b, 0.0)
    joined_real = jnp.concatenate([cols_a[0], cols_b[0]], axis=1)
    joined_imag = jnp.concatenate([cols_a[1], cols_b[1]], axis=1)
    reduced = lax.psum_scatter(
        region_terms(region_inverse, joined_real, joined_imag),
        "pcol",
        scatter_dimension=0,
        tiled=True,
    )
    sum_a = jnp.stack([reduced[:, :width], reduced[:, 2 * width : 3 * width]])
    sum_b = jnp.stack([reduced[:, width : 2 * width], reduced[:, 3 * width :]])
    column_a = -jnp.where(live_mask, sum_a, 0.0)
    column_b = -jnp.where(kept_mask, sum_b + complex_product(column_a, top_full), 0.0)
    term_one = complex_product(flipped(masked_a), column_a)
    term_two = complex_product(flipped(column_a), masked_b)
    term_three = complex_product(flipped(masked_b), column_b)
    total_one, total_two, total_three = lax.psum((term_one, term_two, term_three), ("prow", "pcol"))
    corner_a = full_diag_a - total_one
    top_b = -(complex_product(corner_a, top_full) + total_two)
    corner_b = full_diag_b - complex_product(flipped(top_full), top_b) - total_three
    return (column_a, corner_a, top_b, column_b, corner_b)


def links(move):
    pairs = []
    for row in range(4):
        for col in range(8):
            target = move(row, col // 2, col % 2)
            if target is not None:
                pairs.append((row * 8 + col, target[0] * 8 + target[1] * 2 + target[2]))
    return pairs


def spread_row(row, z, core):
    return row ^ z ^ (3 * core)


CORE = links(lambda row, z, core: (row, z, 1 - core))
UP = links(lambda row, z, core: (row, z + 1, core) if z < 3 else None)
DOWN = links(lambda row, z, core: (row, z - 1, core) if z > 0 else None)
ROW = {m: links(lambda row, z, core, m=m: (row ^ m, z, core)) for m in (1, 2, 3)}
DEPTH = {m: links(lambda row, z, core, m=m: (row, z ^ m, core)) for m in (1, 2, 3)}
SPREAD = links(lambda row, z, core: (spread_row(row, z, core), z, core))
HOME = links(lambda row, z, core: (row, spread_row(row, z, core), z // 2))


def send(block, pairs):
    return lax.ppermute(block, AXES, pairs)


def gather_panel(panel):
    own = send(send(panel, SPREAD), HOME)
    from_x = send(own, ROW[1])
    from_y = send(own, ROW[2])
    far = jnp.stack([send(from_y[0], ROW[1]), send(from_x[1], ROW[2])])
    return [own, from_x, from_y, far]


def shard_positions(row, z, core):
    places = []
    for m in range(4):
        owner = row ^ m ^ z
        source_core = core ^ (owner // 2)
        source_z = owner ^ (3 * source_core)
        places.append(2 * (source_z % 2) + source_core)
    return jnp.stack(places)


def split_weights(shards, mask):
    real = jnp.where(mask, jnp.concatenate([s[0] for s in shards], axis=0), 0.0)
    imag = jnp.where(mask, jnp.concatenate([s[1] for s in shards], axis=0), 0.0)
    parts = []
    for value in (real, imag - real, real + imag):
        head = lax.reduce_precision(value, 8, 7)
        parts.append(jnp.stack([head, value - head]))
    return jnp.stack(parts).astype(jnp.bfloat16)


def product_kernel(tab_ref, r_ref, w_ref, y_ref, split_ref, sums_ref):
    step = pl.program_id(0)
    count = r_ref.shape[1]
    depth = w_ref.shape[2]
    quarter = depth // 4
    width = w_ref.shape[3]
    kept = y_ref.shape[1]
    steps = 6
    offset = tab_ref[2 * steps + step]

    def convert(group, carry):
        source = pl.ds(pl.multiple_of(group * GROUP, GROUP), GROUP)
        target = pl.ds(pl.multiple_of((offset + group) * GROUP, GROUP), GROUP)
        for q in range(4):
            place = pl.multiple_of(tab_ref[3 * steps + q] * quarter, 128)
            lanes = pl.ds(place, quarter)
            real = r_ref[0, source, lanes]
            imag = r_ref[1, source, lanes]
            for k, value in enumerate((real + imag, real, imag)):
                head = value.astype(jnp.bfloat16)
                rest = (value - head.astype(jnp.float32)).astype(jnp.bfloat16)
                split_ref[2 * k, target, q * quarter : (q + 1) * quarter] = head
                split_ref[2 * k + 1, target, q * quarter : (q + 1) * quarter] = rest
        return carry

    lax.fori_loop(0, tab_ref[steps + step], convert, 0)

    @pl.when(step == steps - 1)
    def _():
        total = offset + tab_ref[steps + step]

        def multiply(tile, carry):
            rows = pl.ds(pl.multiple_of(tile * TILE, TILE), TILE)

            def triple(k):
                head = split_ref[2 * k, rows, :]
                rest = split_ref[2 * k + 1, rows, :]
                return (
                    jnp.dot(head, w_ref[k, 0], preferred_element_type=jnp.float32)
                    + jnp.dot(head, w_ref[k, 1], preferred_element_type=jnp.float32)
                    + jnp.dot(rest, w_ref[k, 0], preferred_element_type=jnp.float32)
                )

            first = triple(0)
            sums_ref[rows, width:] = first + triple(1)
            sums_ref[rows, :width] = first - triple(2)
            return carry

        lax.fori_loop(0, (total * GROUP + TILE - 1) // TILE, multiply, 0)
        y_ref[0] = sums_ref[:kept, :]
        middle = pl.multiple_of(tab_ref[2 * steps + 3] * GROUP, GROUP)
        y_ref[1] = sums_ref[pl.ds(middle, kept), :]


TILE = 128


def unit_product(table, region_inverse, weights, kept, flops):
    depth = region_inverse.shape[2]
    width = weights.shape[3]
    half = 3 * BS
    return pl.pallas_call(
        product_kernel,
        out_shape=jax.ShapeDtypeStruct((2, kept, 2 * width), jnp.float32),
        grid_spec=pltpu.PrefetchScalarGridSpec(
            num_scalar_prefetch=1,
            grid=(6,),
            in_specs=[
                pl.BlockSpec((2, BS, depth), lambda i, tab: (0, tab[i], 0)),
                pl.BlockSpec(
                    (3, 2, depth, width),
                    lambda i, tab: (0, 0, 0, 0),
                    pipeline_mode=pl.Buffered(1),
                ),
            ],
            out_specs=pl.BlockSpec((2, kept, 2 * width), lambda i, tab: (0, 0, 0)),
            scratch_shapes=[
                pltpu.VMEM((6, 2 * half, depth), jnp.bfloat16),
                pltpu.VMEM((2 * half, 2 * width), jnp.float32),
            ],
        ),
        compiler_params=pltpu.CompilerParams(dimension_semantics=("arbitrary",)),
        cost_estimate=pl.CostEstimate(
            flops=flops, bytes_accessed=2 * 6 * BS * depth * 4, transcendentals=0
        ),
    )(table, region_inverse, weights)


def unfold_kernel(tab_ref, sum_ref, base_ref, out_ref):
    width = base_ref.shape[2]
    for b in range(3):
        for g in range(BS // GROUP):
            rows = slice(b * BS + g * GROUP, b * BS + (g + 1) * GROUP)
            live = tab_ref[b] > g * GROUP

            @pl.when(live)
            def _():
                start = pl.multiple_of((tab_ref[3 + b] + g) * GROUP, GROUP)
                value = sum_ref[pl.ds(start, GROUP), :]
                line = g * GROUP + lax.broadcasted_iota(jnp.int32, value.shape, 0)
                value = jnp.where(line < tab_ref[b], value, 0.0)
                out_ref[0, rows, :] = -(base_ref[0, rows, :] + value[:, :width])
                out_ref[1, rows, :] = -(base_ref[1, rows, :] + value[:, width:])

            @pl.when(jnp.logical_not(live))
            def _():
                out_ref[0, rows, :] = -base_ref[0, rows, :]
                out_ref[1, rows, :] = -base_ref[1, rows, :]


def unfold(table, total, base):
    return pl.pallas_call(
        unfold_kernel,
        out_shape=jax.ShapeDtypeStruct(base.shape, jnp.float32),
        in_specs=[
            pl.BlockSpec(memory_space=pltpu.SMEM),
            pl.BlockSpec(memory_space=pltpu.VMEM),
            pl.BlockSpec(memory_space=pltpu.VMEM),
        ],
        out_specs=pl.BlockSpec(memory_space=pltpu.VMEM),
        cost_estimate=pl.CostEstimate(
            flops=base.size, bytes_accessed=3 * base.size * 4, transcendentals=0
        ),
    )(table, total, base)


def before(counts):
    size = counts.shape[-1]
    lower = jnp.arange(size)[:, None] > jnp.arange(size)[None, :]
    return jnp.sum(jnp.where(lower, counts[..., None, :], 0), axis=-1)


def unit_tables(heights, order, places):
    blocks = 6 * order[:, None] + jnp.arange(6, dtype=jnp.int32)[None, :]
    catalog = jnp.arange(heights.shape[0], dtype=jnp.int32)
    selector = blocks[:, :, None] == catalog[None, None, :]
    chosen = jnp.sum(jnp.where(selector, heights[None, None, :], 0), axis=-1)
    groups = (chosen + GROUP - 1) // GROUP
    tail = jnp.broadcast_to(places[None, :], (4, 4))
    return jnp.concatenate([blocks, groups, before(groups), tail], axis=1).astype(jnp.int32)


def own_table(heights, position):
    chosen = lax.dynamic_slice_in_dim(heights, 3 * position, 3)
    groups = (chosen + GROUP - 1) // GROUP
    return jnp.concatenate([chosen, before(groups)]).astype(jnp.int32)


def chain_sum(tables, region_inverse, weights, z, core, kept, flops):
    units = []
    for k in range(4):
        product = unit_product(tables[k], region_inverse, weights, kept, flops)
        mine = lax.dynamic_index_in_dim(product, core, 0, keepdims=False)
        other = lax.dynamic_index_in_dim(product, 1 - core, 0, keepdims=False)
        units.append((mine, send(other, CORE)))
    one, two, three, four = [mine + other for mine, other in units]
    up = send(one, UP)
    down = send(one, DOWN)
    up, down = (
        send(jnp.where(z == 0, two, one) + up, UP),
        send(jnp.where(z == 3, two, one) + down, DOWN),
    )
    up, down = (
        send(jnp.where(z == 1, two, three) + up, UP),
        send(jnp.where(z == 2, two, three) + down, DOWN),
    )
    return four + (up + down)


def sum_everywhere(block, row, core):
    half = block.shape[0] // 2
    piece = half // 4
    mine = lax.dynamic_slice_in_dim(block, core * half, half, 0)
    other = lax.dynamic_slice_in_dim(block, (1 - core) * half, half, 0)
    pair = mine + send(other, CORE)
    parts = [lax.dynamic_slice_in_dim(pair, (row ^ m) * piece, piece, 0) for m in range(4)]
    plane = (parts[0] + send(parts[1], ROW[1])) + (send(parts[2], ROW[2]) + send(parts[3], ROW[3]))
    deep = (plane + send(plane, DEPTH[1])) + (send(plane, DEPTH[2]) + send(plane, DEPTH[3]))
    wide = jnp.stack([deep] + [send(deep, ROW[m]) for m in (1, 2, 3)])
    both = jnp.stack([wide, send(wide, CORE)])
    return jnp.concatenate(
        [both[core ^ (q // 4), row ^ (q % 4)] for q in range(8)], axis=0
    )


def cross(left, right):
    joined_left = jnp.concatenate([left[0], left[1]], axis=1)
    joined_right = jnp.concatenate([right[0], right[1]], axis=1)
    width = left.shape[2]
    result = lax.dot_general(
        joined_left,
        joined_right,
        (((0,), (0,)), ((), ())),
        precision=HIGH,
        preferred_element_type=jnp.float32,
    )
    real = result[:width, :width] - result[width:, width:]
    imag = result[:width, width:] + result[width:, :width]
    return jnp.concatenate([real, imag], axis=0)


def apply(left, right):
    joined = jnp.concatenate(
        [
            jnp.concatenate([right[0], right[1]], axis=1),
            jnp.concatenate([-right[1], right[0]], axis=1),
        ],
        axis=0,
    )
    wide = jnp.concatenate([left[0], left[1]], axis=1)
    result = jnp.dot(wide, joined, precision=HIGH, preferred_element_type=jnp.float32)
    width = right.shape[2]
    return jnp.stack([result[:, :width], result[:, width:]])


def on_device(region_inverse, panel_a, panel_b, top_block, diag_a, diag_b, block_rows, struct_b):
    own_rows = panel_a.shape[1]
    width = panel_a.shape[2]
    row = lax.axis_index("prow")
    col = lax.axis_index("pcol")
    z = col // 2
    core = col % 2
    catalog = jnp.arange(block_rows.shape[0], dtype=jnp.int32)
    member = jnp.any(struct_b[:, None] == catalog[None, :], axis=0)
    heights_a = block_rows
    heights_b = jnp.where(member, block_rows, 0)
    row_blocks = region_inverse.shape[1] // BS
    col_blocks = region_inverse.shape[2] // BS
    places = shard_positions(row, z, core)
    ahead = jnp.arange(4, dtype=jnp.int32)
    order = jnp.where(
        z == 0,
        3 - ahead,
        jnp.where(
            z == 3,
            ahead,
            jnp.where(
                z == 1,
                jnp.array([3, 2, 0, 1], jnp.int32),
                jnp.array([0, 1, 3, 2], jnp.int32),
            ),
        ),
    )
    rows_a = lax.dynamic_slice_in_dim(heights_a, row * row_blocks, row_blocks)
    rows_b = lax.dynamic_slice_in_dim(heights_b, row * row_blocks, row_blocks)
    tables_a = unit_tables(rows_a, order, places)
    tables_b = unit_tables(rows_b, order, places)
    own_a = own_table(rows_a, col)
    own_b = own_table(rows_b, col)

    def col_mask(heights):
        part = lax.dynamic_slice_in_dim(heights, col * col_blocks, col_blocks).reshape(4, -1)
        part = jnp.concatenate(
            [lax.dynamic_slice_in_dim(part, places[m], 1, 0) for m in range(4)], axis=0
        )
        inside = jnp.arange(BS, dtype=jnp.int32)[None, :] < part.reshape(-1, 1)
        return inside.reshape(-1, 1)

    def own_mask(table):
        inside = jnp.arange(BS, dtype=jnp.int32)[None, :] < table[:3, None]
        return inside.reshape(1, own_rows, 1)

    cost = 2 * 6 * BS * region_inverse.shape[2] * width * 6
    weights_a = split_weights(gather_panel(panel_a), col_mask(heights_a))
    top_pieces = [top_block] + [send(top_block, DEPTH[m]) for m in (1, 2, 3)]
    top_pieces = jnp.stack(top_pieces)
    top_pieces = jnp.stack([top_pieces, send(top_pieces, CORE)])
    top_full = jnp.concatenate(
        [top_pieces[core ^ (q % 2), z ^ (q // 2)] for q in range(8)], axis=1
    )
    sum_a = chain_sum(tables_a, region_inverse, weights_a, z, core, own_rows, cost)
    weights_b = split_weights(gather_panel(panel_b), col_mask(heights_b))
    sum_b = chain_sum(tables_b, region_inverse, weights_b, z, core, own_rows, cost // 3)
    live_mask = own_mask(own_a)
    kept_mask = own_mask(own_b)
    masked_a = jnp.where(live_mask, panel_a, 0.0)
    masked_b = jnp.where(kept_mask, panel_b, 0.0)
    column_a = unfold(own_a, sum_a, jnp.zeros_like(panel_a))
    base_b = jnp.where(kept_mask, apply(column_a, top_full), 0.0)
    lead = jnp.where(row == 0, 1.0, 0.0)

    def placed(diag):
        empty = jnp.zeros((2, width, width), jnp.float32)
        slab = lax.dynamic_update_slice_in_dim(empty, diag * lead, col * diag.shape[1], 1)
        return slab.reshape(2 * width, width)

    early = jnp.concatenate(
        [placed(diag_a) - cross(masked_a, column_a), cross(column_a, masked_b)], axis=0
    )
    early = sum_everywhere(early, row, core)
    corner_a = early[: 2 * width].reshape(2, width, width)
    term_two = early[2 * width :].reshape(2, width, width)
    top_b = -(apply(corner_a, top_full) + term_two)
    lower = apply(flipped(top_full), top_b)
    column_b = unfold(own_b, sum_b, base_b)
    late = placed(diag_b) - cross(masked_b, column_b)
    late = sum_everywhere(late, row, core).reshape(2, width, width)
    corner_b = late - lower
    return (column_a, corner_a, top_b, column_b, corner_b)


def solution(mesh):
    in_specs = (
        P(None, "prow", "pcol"),
        P(None, ("prow", "pcol"), None),
        P(None, ("prow", "pcol"), None),
        P(None, "pcol", None),
        P(None, "pcol", None),
        P(None, "pcol", None),
        P(),
        P(),
    )
    out_specs = (P(None, ("prow", "pcol"), None), P(), P(), P(None, ("prow", "pcol"), None), P())
    small = mesh.shape["prow"] == 4 and mesh.shape["pcol"] == 8
    return jax.shard_map(
        on_device if small else on_device_generic,
        mesh=mesh,
        in_specs=in_specs,
        out_specs=out_specs,
        check_vma=False,
    )
```
